32 devices in a mesh: patch: 16 (over z, y, core), chan: 2 (over x).
Axes of the slice: x: 2, y: 2, z: 4, core: 2. Of those that a mesh axis runs over, the one named last changes fastest.
Arguments:
- fields: bfloat16 [16, 128, 1024], P('patch', 'chan'), may hold values from -6 to 6
- w_one: bfloat16 [9, 512, 128], P(None, 'chan'), may hold values from -0.1875 to 0.1875
- bias_one: float32 [512], P('chan'), may hold values from -3 to 3
- w_two: bfloat16 [9, 128, 512], P(None, None, 'chan'), may hold values from -0.09375 to 0.09375
- neighbour: int32 [16, 4], replicated, may hold values from 0 to 15, as said below
- seam_code: int32 [16, 4], replicated, may hold values from 0 to 7, as said below
- band_order: int32 [16], replicated, may hold values from 0 to 15, each once
- target: bfloat16 [16, 128, 1024], P('patch', 'chan'), may hold values from -6 to 6
- lat_weight: bfloat16 [16, 1024], P('patch'), may hold values from 0.099609375 to 1
Outputs:
- loss_value: float32 [], replicated
- grad_one: float32 [9, 512, 128], P(None, 'chan')
- grad_two: float32 [9, 128, 512], P(None, None, 'chan')
- grad_bias: float32 [512], P('chan')
The draws below stay inside these ranges and needn't reach their ends.
Inputs may be any that keep to these rules, and one draw needn't show every extreme that they name: The sides of all patches are paired: side s of patch p borders side t = seam_code[p, s] mod 4 of patch q = neighbour[p, s], and then neighbour[q, t] = p, seam_code[q, t] mod 4 = s, and both codes agree on being 4 or more; so every edge is read by exactly one side of one other patch, and the four sides of a patch face four different patches. `seam_code`: code mod 4 names the neighbour's edge that forms the seam; codes 4 and above run that edge reversed, alike on both sides of a seam. `band_order`: each patch fills exactly one slot of every band.
All inputs are finite; a program needn't handle non-finite values.
Results may differ from the reference program's by a relative error of at most 0.0021.
Values may be sent and summed in bfloat16 or wider, within the bound.
A program may use at most 64 MiB of HBM per device.

```python
import math
import jax
import jax.numpy as jnp
from jax import lax

C = 128
E = 512
P_SIZE = 32
PATCHES = 16


def adjacency(key):
    count = PATCHES
    base = jax.random.fold_in(key, 7)
    key_order, key_offset, key_sides, key_east, key_south = jax.random.split(base, 5)
    order = jax.random.permutation(key_order, count).astype(jnp.int32)
    offset = jax.random.randint(key_offset, (), 2, count // 2).astype(jnp.int32)
    side_keys = jax.random.split(key_sides, count)
    labels = jax.vmap(lambda one_key: jax.random.permutation(one_key, 4))(side_keys).astype(jnp.int32)
    flip_east = jax.random.randint(key_east, (count,), 0, 2).astype(jnp.int32)
    flip_south = jax.random.randint(key_south, (count,), 0, 2).astype(jnp.int32)
    places = jnp.arange(count, dtype=jnp.int32)
    north_at = (places - offset) % count
    south_at = (places + offset) % count
    west_at = (places - 1) % count
    east_at = (places + 1) % count
    partners = jnp.stack([order[north_at], order[south_at], order[west_at], order[east_at]], axis=1)
    flips = jnp.stack([flip_south[north_at], flip_south, flip_east[west_at], flip_east], axis=1)
    partner_logical = jnp.array([1, 0, 3, 2], dtype=jnp.int32)
    partner_side = labels[partners, partner_logical[None, :]]
    codes = partner_side + 4 * flips
    own_side = labels[order]
    rows = jnp.broadcast_to(order[:, None], (count, 4))
    neighbour = jnp.zeros((count, 4), jnp.int32).at[rows, own_side].set(partners)
    seam_code = jnp.zeros((count, 4), jnp.int32).at[rows, own_side].set(codes)
    return (neighbour, seam_code)


def draw_neighbour(key, part):
    return adjacency(key)[0]


def draw_seam_code(key, part):
    return adjacency(key)[1]


def shard_levels(key, extent, cuts, smallest, top_value):
    def one(position, parts):
        heights = jax.random.uniform(jax.random.fold_in(jax.random.fold_in(key, 6), position), (parts,), jnp.float32, smallest / len(cuts), top_value / len(cuts))
        return jnp.repeat(jnp.exp(heights), extent[position] // parts).reshape((-1,) + (1,) * (len(extent) - position - 1))

    loudness = one(*cuts[0])
    for cut in cuts[1:]:
        loudness = loudness * one(*cut)
    return loudness


def gaussian(own_key, dims, spread, limit, pieces=(), held_as=jnp.bfloat16):
    values = spread * jax.random.normal(own_key, dims, jnp.float32)
    if pieces:
        values = values * shard_levels(own_key, dims, pieces, -0.22, 0.18)
    return jnp.clip(values, -limit, limit).astype(held_as)


def setup_inputs(seed: int = 0) -> dict:
    arg_keys = jax.random.split(jax.random.key(seed), 10)
    return {
        "fields": gaussian(arg_keys[0], (PATCHES, C, P_SIZE * P_SIZE), 1.0, 6.0, ((0, 16), (1, 2))),
        "w_one": gaussian(arg_keys[1], (9, E, C), (9 * C) ** -0.5, 0.1875, ((1, 2),)),
        "bias_one": gaussian(arg_keys[2], (E,), 0.5, 3.0, ((0, 2),), jnp.float32),
        "w_two": gaussian(arg_keys[3], (9, C, E), (9 * E) ** -0.5, 0.09375, ((2, 2),)),
        "neighbour": draw_neighbour(jax.random.fold_in(arg_keys[9], 71), 0),
        "seam_code": draw_seam_code(jax.random.fold_in(arg_keys[9], 71), 0),
        "band_order": jax.random.permutation(arg_keys[6], PATCHES).astype(jnp.int32),
        "target": gaussian(arg_keys[7], (PATCHES, C, P_SIZE * P_SIZE), 1.0, 6.0, ((0, 16), (1, 2))),
        "lat_weight": jnp.clip(jnp.exp(math.log(1.0) - 2.306499 * jax.random.uniform(arg_keys[8], (PATCHES, P_SIZE * P_SIZE), jnp.float32) ** shard_levels(arg_keys[8], (PATCHES, P_SIZE * P_SIZE), ((0, 16),), -0.2, 0.2)), 0.099609375, 1.0).astype(jnp.bfloat16),
    }


def edges_of(field):
    return jnp.stack([field[..., 0, :], field[..., -1, :], field[..., :, 0], field[..., :, -1]], axis=-3)

def frames_for(edge_all, neighbour, seam_code):
    picked = edge_all[neighbour, seam_code % 4]
    return jnp.where((seam_code >= 4)[:, :, None, None], picked[..., ::-1], picked)

def with_frame(field, strips):
    padded = jnp.pad(field, ((0, 0), (1, 1), (1, 1)))
    padded = padded.at[:, 0, 1:-1].set(strips[0])
    padded = padded.at[:, -1, 1:-1].set(strips[1])
    padded = padded.at[:, 1:-1, 0].set(strips[2])
    padded = padded.at[:, 1:-1, -1].set(strips[3])
    return padded

def tap_list(padded):
    length = padded.shape[-1] - 2
    return [padded[:, row_off:row_off + length, col_off:col_off + length].reshape(padded.shape[0], length * length) for row_off in range(3) for col_off in range(3)]

def apply_taps(weight, taps):
    summed = jnp.zeros((weight.shape[1], taps[0].shape[1]), jnp.float32)
    for tap_index in range(9):
        summed = summed + jnp.dot(weight[tap_index], taps[tap_index], preferred_element_type=jnp.float32)
    return summed

def smooth_gate(values):
    return jax.nn.gelu(values, approximate=True)

def reference(fields, w_one, bias_one, w_two, neighbour, seam_code, band_order, target, lat_weight):
    patch_count = fields.shape[0]
    cell_count = P_SIZE * P_SIZE
    part_len = cell_count // patch_count
    grid = fields.reshape(patch_count, C, P_SIZE, P_SIZE)
    frame_x = frames_for(edges_of(grid), neighbour, seam_code)

    def first_layer(inputs_row):
        field, strips = inputs_row
        preact = apply_taps(w_one, tap_list(with_frame(field, strips))) + bias_one[:, None]
        return smooth_gate(preact).astype(jnp.bfloat16)
    hidden = lax.map(first_layer, (grid, frame_x))
    hidden_grid = hidden.reshape(patch_count, E, P_SIZE, P_SIZE)
    frame_h = frames_for(edges_of(hidden_grid), neighbour, seam_code)

    def second_layer(inputs_row):
        field_row, hfield, strips = inputs_row
        return field_row.astype(jnp.float32) + apply_taps(w_two, tap_list(with_frame(hfield, strips)))
    outputs = lax.map(second_layer, (fields, hidden_grid, frame_h))
    inverse = jnp.zeros((patch_count,), jnp.int32).at[band_order].set(jnp.arange(patch_count, dtype=jnp.int32))
    tgt = target.reshape(patch_count, C, patch_count, part_len)[:, :, inverse, :]
    tgt = jnp.transpose(tgt, (2, 1, 0, 3)).reshape(patch_count, C, cell_count)
    lat_w = lat_weight.reshape(patch_count, patch_count, part_len)[:, inverse, :]
    lat_w = jnp.transpose(lat_w, (1, 0, 2)).reshape(patch_count, 1, cell_count).astype(jnp.float32)
    misfit = outputs - tgt.astype(jnp.float32)
    loss_value = jnp.sum(lat_w * misfit * misfit) / (patch_count * cell_count * C)
    inv_root = 1.0 / math.sqrt(patch_count * cell_count)
    grad_out = (lat_w * misfit * inv_root).astype(jnp.bfloat16)

    def transpose_layer(gout):
        gpad = jnp.zeros((E, P_SIZE + 2, P_SIZE + 2), jnp.float32)
        tap_index = 0
        for row_off in range(3):
            for col_off in range(3):
                block = jnp.dot(w_two[tap_index].T, gout, preferred_element_type=jnp.float32).reshape(E, P_SIZE, P_SIZE)
                gpad = gpad + jnp.pad(block, ((0, 0), (row_off, 2 - row_off), (col_off, 2 - col_off)))
                tap_index = tap_index + 1
        frames = jnp.stack([gpad[:, 0, 1:-1], gpad[:, -1, 1:-1], gpad[:, 1:-1, 0], gpad[:, 1:-1, -1]])
        return (gpad[:, 1:-1, 1:-1], frames)
    interior, frames = lax.map(transpose_layer, grad_out)
    turned = jnp.where((seam_code >= 4)[:, :, None, None], frames[..., ::-1], frames)
    back = jax.ops.segment_sum(turned.reshape(patch_count * 4, E, P_SIZE), (neighbour * 4 + seam_code % 4).reshape(-1), num_segments=patch_count * 4).reshape(patch_count, 4, E, P_SIZE)

    def accumulate(carry, inputs_row):
        acc_one, acc_two, acc_bias = carry
        field, xstrips, hfield, hstrips, inner, edge_back, gout = inputs_row
        x_taps = tap_list(with_frame(field, xstrips))
        preact = apply_taps(w_one, x_taps) + bias_one[:, None]
        grad_h = inner.at[:, 0, :].add(edge_back[0])
        grad_h = grad_h.at[:, -1, :].add(edge_back[1])
        grad_h = grad_h.at[:, :, 0].add(edge_back[2])
        grad_h = grad_h.at[:, :, -1].add(edge_back[3])
        grad_h = grad_h.reshape(E, cell_count)
        grad_pre = jax.vjp(smooth_gate, preact)[1](grad_h)[0]
        pre_b = grad_pre.astype(jnp.bfloat16)
        h_taps = tap_list(with_frame(hfield, hstrips))
        acc_one = acc_one + jnp.stack([jnp.dot(pre_b, x_taps[idx].T, preferred_element_type=jnp.float32) for idx in range(9)])
        acc_two = acc_two + jnp.stack([jnp.dot(gout, h_taps[idx].T, preferred_element_type=jnp.float32) for idx in range(9)])
        acc_bias = acc_bias + lax.optimization_barrier(jnp.sum(grad_pre, axis=1))
        return ((acc_one, acc_two, acc_bias), None)
    start_val = (jnp.zeros((9, E, C), jnp.float32), jnp.zeros((9, C, E), jnp.float32), jnp.zeros((E,), jnp.float32))
    (grad_one, grad_two, grad_bias), _ = lax.scan(accumulate, start_val, (grid, frame_x, hidden_grid, frame_h, interior, back, grad_out))
    return (loss_value, grad_one, grad_two, grad_bias)
```

```python
import math

import jax
import jax.numpy as jnp
from jax import lax
from jax.sharding import PartitionSpec as P

P_SIZE = 32


def edges_of(grid):
    return jnp.stack([grid[0], grid[-1], grid[:, 0], grid[:, -1]])


def with_frame(grid, strips):
    rows = jnp.concatenate([strips[0][None], grid, strips[1][None]], axis=0)
    left = jnp.pad(strips[2], ((1, 1), (0, 0)))[:, None]
    right = jnp.pad(strips[3], ((1, 1), (0, 0)))[:, None]
    return jnp.concatenate([left, rows, right], axis=1)


def conv(values, weight, pad, spec):
    return lax.conv_general_dilated(
        values[None],
        weight,
        (1, 1),
        ((pad, pad), (pad, pad)),
        dimension_numbers=("NHWC", spec, "NHWC"),
        preferred_element_type=jnp.float32,
    )[0]


def smooth_gate(values):
    return jax.nn.gelu(values, approximate=True)


def on_device(fields, w_one, bias_one, w_two, neighbour, seam_code, band_order, target, lat_weight):
    length = P_SIZE
    cells = length * length
    count = lax.axis_size("patch")
    chans = lax.axis_size("chan")
    part = cells // count
    own = lax.axis_index("patch")
    own_nbr = lax.dynamic_slice_in_dim(neighbour, own, 1, 0)[0]
    own_code = lax.dynamic_slice_in_dim(seam_code, own, 1, 0)[0]
    ids = jnp.arange(count, dtype=jnp.int32)
    faces = (own_nbr[:, None] == ids[None, :]).astype(jnp.bfloat16)
    turned = (own_code >= 4)[:, None, None]
    inner = w_one.shape[1]

    def to_send(grid):
        strips = edges_of(grid)
        strips = jnp.where(turned, strips[:, ::-1], strips)
        return jnp.einsum(
            "tr,tkc->rkc", faces, strips, preferred_element_type=jnp.float32
        ).astype(jnp.bfloat16)

    def picked(arrived):
        return jnp.einsum(
            "tr,rkc->tkc", faces, arrived, preferred_element_type=jnp.float32
        ).astype(jnp.bfloat16)

    def swap(sent):
        return lax.all_to_all(sent, "patch", split_axis=0, concat_axis=0, tiled=True)

    both = lax.all_gather(jnp.stack([fields[0], target[0]]), "chan", axis=1, tiled=True)
    chan_full = both.shape[1]
    x_grid = both[0].T.reshape(length, length, chan_full)
    slots = (band_order[None, :] == ids[:, None]).astype(jnp.bfloat16)
    lat_rows = -(-part // chan_full)
    lat_parts = jnp.pad(
        lat_weight.reshape(count, part), ((0, 0), (0, lat_rows * chan_full - part))
    ).reshape(count, lat_rows, chan_full)
    band_parts = jnp.concatenate(
        [both[1].T.reshape(count, part, chan_full), lat_parts], axis=1
    )
    band_parts = jnp.einsum(
        "ps,skc->pkc", slots, band_parts, preferred_element_type=jnp.float32
    ).astype(jnp.bfloat16)
    first = swap(jnp.concatenate([to_send(x_grid), band_parts], axis=1))
    x_pad = with_frame(x_grid, picked(first[:, :length]))
    target_patch = first[:, length : length + part].reshape(cells, chan_full)
    lat_w = (
        first[:, length + part :].reshape(count, lat_rows * chan_full)[:, :part].reshape(cells, 1)
    ).astype(jnp.float32)

    preact = conv(x_pad, w_one.reshape(3, 3, inner, chan_full), 0, "HWOI") + bias_one
    hidden = smooth_gate(preact).astype(jnp.bfloat16)
    h_pad = with_frame(hidden, picked(swap(to_send(hidden))))
    partial = conv(h_pad, w_two.reshape(3, 3, chan_full, inner), 0, "HWOI").reshape(
        cells, chan_full
    )
    mixed = partial
    rounded = partial.astype(jnp.bfloat16)
    for shift in range(1, chans):
        mixed = mixed + lax.ppermute(
            rounded, "chan", [(i, (i + shift) % chans) for i in range(chans)]
        ).astype(jnp.float32)
    x_flat = x_grid.reshape(cells, chan_full)
    misfit = x_flat.astype(jnp.float32) + mixed - target_patch.astype(jnp.float32)
    weighted = lat_w * misfit
    loss_local = jnp.sum(weighted * misfit)
    inv_root = 1.0 / math.sqrt(count * cells)
    grad_out = (weighted * inv_root).astype(jnp.bfloat16)
    g_grid = grad_out.reshape(length, length, chan_full)

    h_taps = [
        h_pad[a : a + length, b : b + length].reshape(cells, inner)
        for a in range(3)
        for b in range(3)
    ]
    two_local = jnp.stack(
        [
            lax.dot_general(
                grad_out, tap, (((0,), (0,)), ((), ())), preferred_element_type=jnp.float32
            )
            for tap in h_taps
        ]
    )

    near = picked(swap(to_send(g_grid)))
    side_taps = jnp.array([[0, 1, 2], [6, 7, 8], [0, 3, 6], [2, 5, 8]], jnp.int32)
    used = side_taps[own_code % 4]
    used = jnp.where((own_code >= 4)[:, None], used[:, ::-1], used)
    hot = (used[:, :, None] == jnp.arange(9)[None, None, :]).astype(jnp.bfloat16)
    spread = jnp.pad(near, ((0, 0), (1, 1), (0, 0)))
    shifted = jnp.stack([spread[:, 2 - d : 2 - d + length] for d in range(3)], axis=1)
    side_in = jnp.einsum(
        "tdn,tdkc->tknc", hot, shifted, preferred_element_type=jnp.float32
    ).astype(jnp.bfloat16)
    back = lax.dot_general(
        side_in.reshape(4 * length, 9 * chan_full),
        w_two.reshape(9 * chan_full, inner),
        (((1,), (0,)), ((), ())),
        preferred_element_type=jnp.float32,
    ).reshape(4, length, inner)
    grad_h = conv(g_grid, w_two.reshape(3, 3, chan_full, inner)[::-1, ::-1], 1, "HWIO")
    row = lax.broadcasted_iota(jnp.int32, (length, length, 1), 0)
    col = lax.broadcasted_iota(jnp.int32, (length, length, 1), 1)
    grad_h = (
        grad_h
        + jnp.where(row == 0, back[0][None], 0.0)
        + jnp.where(row == length - 1, back[1][None], 0.0)
        + jnp.where(col == 0, back[2][:, None], 0.0)
        + jnp.where(col == length - 1, back[3][:, None], 0.0)
    )
    grad_pre = jax.vjp(smooth_gate, preact)[1](grad_h)[0].reshape(cells, inner)
    bias_local = jnp.sum(grad_pre, axis=0)
    pre_b = grad_pre.astype(jnp.bfloat16)
    x_taps = [
        x_pad[a : a + length, b : b + length].reshape(cells, chan_full)
        for a in range(3)
        for b in range(3)
    ]
    one_local = jnp.stack(
        [
            lax.dot_general(
                pre_b, tap, (((0,), (0,)), ((), ())), preferred_element_type=jnp.float32
            )
            for tap in x_taps
        ]
    )
    small_rows = -(-inner // chan_full) + 1
    small = jnp.concatenate(
        [
            jnp.pad(bias_local, (0, (small_rows - 1) * chan_full - inner)),
            jnp.pad(loss_local[None], (0, chan_full - 1)),
        ]
    ).reshape(small_rows, chan_full)
    sum_two = lax.psum(two_local, "patch")
    sums = lax.psum(
        jnp.concatenate([one_local.reshape(9 * inner, chan_full), small], axis=0), "patch"
    )
    grad_one = sums[: 9 * inner].reshape(9, inner, chan_full)
    grad_bias = sums[9 * inner : -1].reshape(-1)[:inner]
    loss_value = sums[-1, 0] / (count * cells * chan_full)
    return (loss_value, grad_one, sum_two, grad_bias)


def solution(mesh):
    placed = (
        P("patch", "chan", None),
        P(None, "chan", None),
        P("chan"),
        P(None, None, "chan"),
        P(),
        P(),
        P(),
        P("patch", "chan", None),
        P("patch", None),
    )
    return jax.shard_map(
        on_device,
        mesh=mesh,
        in_specs=placed,
        out_specs=(P(), P(None, "chan", None), P(None, None, "chan"), P("chan")),
        check_vma=False,
    )
```

```python
import math

import jax
import jax.numpy as jnp
from jax import lax
from jax.experimental import pallas as pl
from jax.experimental.pallas import tpu as pltpu
from jax.sharding import PartitionSpec as P

P_SIZE = 32


def edges_of(grid):
    return jnp.stack([grid[0], grid[-1], grid[:, 0], grid[:, -1]])


def with_frame(grid, strips):
    rows = jnp.concatenate([strips[0][None], grid, strips[1][None]], axis=0)
    left = jnp.pad(strips[2], ((1, 1), (0, 0)))[:, None]
    right = jnp.pad(strips[3], ((1, 1), (0, 0)))[:, None]
    return jnp.concatenate([left, rows, right], axis=1)


def conv(values, weight, pad, spec):
    return lax.conv_general_dilated(
        values[None],
        weight,
        (1, 1),
        ((pad, pad), (pad, pad)),
        dimension_numbers=("NHWC", spec, "NHWC"),
        preferred_element_type=jnp.float32,
    )[0]


def smooth_gate(values):
    return jax.nn.gelu(values, approximate=True)


def bits_of(size):
    return [1 << k for k in range(size.bit_length() - 1)]


def peer_of(place, bit):
    return place + bit - 2 * bit * (lax.div(place, bit) % 2)


def sum_kernel(count, chans, a_in, b_in, s_in, a_out, b_out, s_out, a_rec, b_rec, s_rec, send, recv):
    place = lax.axis_index("patch")
    lane = lax.axis_index("chan")
    bits = bits_of(count)
    swapped = bits if len(bits) < 3 else [bits[0], bits[2], bits[1]] + bits[3:]
    chan_bits = bits_of(chans)
    stages = len(bits)

    def target(bit):
        return {"patch": peer_of(place, bit)}

    barrier = pltpu.get_barrier_semaphore()
    for bit in bits:
        pl.semaphore_signal(
            barrier, inc=1, device_id=target(bit), device_id_type=pl.DeviceIdType.MESH
        )
    for bit in chan_bits:
        pl.semaphore_signal(
            barrier,
            inc=1,
            device_id={"chan": peer_of(lane, bit)},
            device_id_type=pl.DeviceIdType.MESH,
        )
    pl.semaphore_wait(barrier, stages + len(chan_bits))

    slot = [0]

    def send_to(src, dst, device):
        k = slot[0]
        slot[0] = k + 1
        copy = pltpu.make_async_remote_copy(
            src_ref=src,
            dst_ref=dst,
            send_sem=send.at[k],
            recv_sem=recv.at[k],
            device_id=device,
            device_id_type=pl.DeviceIdType.MESH,
        )
        copy.start()
        return copy

    s_out[...] = s_in[...]
    streams = [
        {"in": a_in, "out": a_out, "rec": a_rec, "order": bits, "start": 0},
        {"in": b_in, "out": b_out, "rec": b_rec, "order": swapped, "start": 0},
    ]
    for one in streams:
        one["rows"] = one["in"].shape[0]
        one["base"] = 0
        one["held"] = one["in"]
        one["at"] = 0
    for stage in range(stages):
        flights = []
        for one in streams:
            bit = one["order"][stage]
            half = one["rows"] // 2
            mine = lax.div(place, bit) % 2
            away = pl.multiple_of(one["at"] + (1 - mine) * half, 8)
            landing = one["rec"].at[pl.ds(one["base"], half)]
            flights.append(send_to(one["held"].at[pl.ds(away, half)], landing, target(bit)))
            one["at"] = pl.multiple_of(one["at"] + mine * half, 8)
            one["start"] = one["start"] + mine * half
            one["rows"] = half
        small = send_to(s_out, s_rec.at[stage], target(bits[stage]))
        for one, copy in zip(streams, flights):
            copy.wait()
            half = one["rows"]
            total = one["held"][pl.ds(one["at"], half)] + one["rec"][pl.ds(one["base"], half)]
            if stage == stages - 1:
                one["out"][pl.ds(pl.multiple_of(one["start"], 8), half)] = total
            else:
                one["rec"][pl.ds(one["base"], half)] = total
            one["held"] = one["rec"]
            one["at"] = one["base"]
            one["base"] += half
        small.wait()
        s_out[...] = s_out[...] + s_rec[stage]
    loss_row = lax.broadcasted_iota(jnp.int32, s_out.shape, 0) == s_out.shape[0] - 1
    for stage in range(stages - 1, -1, -1):
        flights = []
        for one in streams:
            bit = one["order"][stage]
            mine = lax.div(place, bit) % 2
            rows = one["rows"]
            part = one["out"].at[pl.ds(pl.multiple_of(one["start"], 8), rows)]
            flights.append(send_to(part, part, target(bit)))
            one["start"] = one["start"] - mine * rows
            one["rows"] = 2 * rows
        behind = stages - 1 - stage
        if behind < len(chan_bits):
            small = send_to(
                s_out, s_rec.at[stages + behind], {"chan": peer_of(lane, chan_bits[behind])}
            )
            small.wait()
            s_out[...] = s_out[...] + jnp.where(loss_row, s_rec[stages + behind], 0.0)
        for copy in flights:
            copy.wait()


def sum_over_patches(a, b, small):
    count = lax.axis_size("patch")
    chans = lax.axis_size("chan")
    stages = len(bits_of(count))
    chan_stages = len(bits_of(chans))
    unit = 8 * count

    def padded(rows):
        return -(-rows // unit) * unit

    a_rows, b_rows = padded(a.shape[0]), padded(b.shape[0])
    a_full = jnp.pad(a, ((0, a_rows - a.shape[0]), (0, 0)))
    b_full = jnp.pad(b, ((0, b_rows - b.shape[0]), (0, 0)))
    copies = 5 * stages + chan_stages
    spec = pl.BlockSpec(memory_space=pltpu.VMEM)

    def kernel(*refs):
        sum_kernel(count, chans, *refs)

    a_sum, b_sum, s_sum = pl.pallas_call(
        kernel,
        out_shape=[
            jax.ShapeDtypeStruct(a_full.shape, jnp.float32),
            jax.ShapeDtypeStruct(b_full.shape, jnp.float32),
            jax.ShapeDtypeStruct(small.shape, jnp.float32),
        ],
        in_specs=[spec] * 3,
        out_specs=[spec] * 3,
        scratch_shapes=[
            pltpu.VMEM((a_rows - 8, a.shape[1]), jnp.float32),
            pltpu.VMEM((b_rows - 8, b.shape[1]), jnp.float32),
            pltpu.VMEM((stages + chan_stages,) + small.shape, jnp.float32),
            pltpu.SemaphoreType.DMA((copies,)),
            pltpu.SemaphoreType.DMA((copies,)),
        ],
        compiler_params=pltpu.CompilerParams(
            collective_id=0, has_side_effects=True, vmem_limit_bytes=24 << 20
        ),
    )(a_full, b_full, small)
    return a_sum[: a.shape[0]], b_sum[: b.shape[0]], s_sum


def on_device(fields, w_one, bias_one, w_two, neighbour, seam_code, band_order, target, lat_weight):
    length = P_SIZE
    cells = length * length
    count = lax.axis_size("patch")
    chans = lax.axis_size("chan")
    part = cells // count
    own = lax.axis_index("patch")
    own_nbr = lax.dynamic_slice_in_dim(neighbour, own, 1, 0)[0]
    own_code = lax.dynamic_slice_in_dim(seam_code, own, 1, 0)[0]
    ids = jnp.arange(count, dtype=jnp.int32)
    faces = (own_nbr[:, None] == ids[None, :]).astype(jnp.bfloat16)
    turned = (own_code >= 4)[:, None, None]
    inner = w_one.shape[1]

    def to_send(grid):
        strips = edges_of(grid)
        strips = jnp.where(turned, strips[:, ::-1], strips)
        return jnp.einsum(
            "tr,tkc->rkc", faces, strips, preferred_element_type=jnp.float32
        ).astype(jnp.bfloat16)

    def picked(arrived):
        return jnp.einsum(
            "tr,rkc->tkc", faces, arrived, preferred_element_type=jnp.float32
        ).astype(jnp.bfloat16)

    def swap(sent):
        return lax.all_to_all(sent, "patch", split_axis=0, concat_axis=0, tiled=True)

    both = lax.all_gather(jnp.stack([fields[0], target[0]]), "chan", axis=1, tiled=True)
    chan_full = both.shape[1]
    x_grid = both[0].T.reshape(length, length, chan_full)
    slots = (band_order[None, :] == ids[:, None]).astype(jnp.bfloat16)
    lat_rows = -(-part // chan_full)
    lat_parts = jnp.pad(
        lat_weight.reshape(count, part), ((0, 0), (0, lat_rows * chan_full - part))
    ).reshape(count, lat_rows, chan_full)
    band_parts = jnp.concatenate(
        [both[1].T.reshape(count, part, chan_full), lat_parts], axis=1
    )
    band_parts = jnp.einsum(
        "ps,skc->pkc", slots, band_parts, preferred_element_type=jnp.float32
    ).astype(jnp.bfloat16)
    first = swap(jnp.concatenate([to_send(x_grid), band_parts], axis=1))
    x_pad = with_frame(x_grid, picked(first[:, :length]))
    target_patch = first[:, length : length + part].reshape(cells, chan_full)
    lat_w = (
        first[:, length + part :].reshape(count, lat_rows * chan_full)[:, :part].reshape(cells, 1)
    ).astype(jnp.float32)

    preact = conv(x_pad, w_one.reshape(3, 3, inner, chan_full), 0, "HWOI") + bias_one
    hidden = smooth_gate(preact).astype(jnp.bfloat16)
    h_pad = with_frame(hidden, picked(swap(to_send(hidden))))
    partial = conv(h_pad, w_two.reshape(3, 3, chan_full, inner), 0, "HWOI").reshape(
        cells, chan_full
    )
    mixed = partial
    rounded = partial.astype(jnp.bfloat16)
    for shift in range(1, chans):
        mixed = mixed + lax.ppermute(
            rounded, "chan", [(i, (i + shift) % chans) for i in range(chans)]
        ).astype(jnp.float32)
    x_flat = x_grid.reshape(cells, chan_full)
    misfit = x_flat.astype(jnp.float32) + mixed - target_patch.astype(jnp.float32)
    weighted = lat_w * misfit
    loss_local = jnp.sum(weighted * misfit)
    inv_root = 1.0 / math.sqrt(count * cells)
    grad_out = (weighted * inv_root).astype(jnp.bfloat16)
    g_grid = grad_out.reshape(length, length, chan_full)

    h_taps = [
        h_pad[a : a + length, b : b + length].reshape(cells, inner)
        for a in range(3)
        for b in range(3)
    ]
    two_local = jnp.stack(
        [
            lax.dot_general(
                grad_out, tap, (((0,), (0,)), ((), ())), preferred_element_type=jnp.float32
            )
            for tap in h_taps
        ]
    )

    near = picked(swap(to_send(g_grid)))
    side_taps = jnp.array([[0, 1, 2], [6, 7, 8], [0, 3, 6], [2, 5, 8]], jnp.int32)
    used = side_taps[own_code % 4]
    used = jnp.where((own_code >= 4)[:, None], used[:, ::-1], used)
    hot = (used[:, :, None] == jnp.arange(9)[None, None, :]).astype(jnp.bfloat16)
    spread = jnp.pad(near, ((0, 0), (1, 1), (0, 0)))
    shifted = jnp.stack([spread[:, 2 - d : 2 - d + length] for d in range(3)], axis=1)
    side_in = jnp.einsum(
        "tdn,tdkc->tknc", hot, shifted, preferred_element_type=jnp.float32
    ).astype(jnp.bfloat16)
    back = lax.dot_general(
        side_in.reshape(4 * length, 9 * chan_full),
        w_two.reshape(9 * chan_full, inner),
        (((1,), (0,)), ((), ())),
        preferred_element_type=jnp.float32,
    ).reshape(4, length, inner)
    grad_h = conv(g_grid, w_two.reshape(3, 3, chan_full, inner)[::-1, ::-1], 1, "HWIO")
    row = lax.broadcasted_iota(jnp.int32, (length, length, 1), 0)
    col = lax.broadcasted_iota(jnp.int32, (length, length, 1), 1)
    grad_h = (
        grad_h
        + jnp.where(row == 0, back[0][None], 0.0)
        + jnp.where(row == length - 1, back[1][None], 0.0)
        + jnp.where(col == 0, back[2][:, None], 0.0)
        + jnp.where(col == length - 1, back[3][:, None], 0.0)
    )
    grad_pre = jax.vjp(smooth_gate, preact)[1](grad_h)[0].reshape(cells, inner)
    bias_local = jnp.sum(grad_pre, axis=0)
    pre_b = grad_pre.astype(jnp.bfloat16)
    x_taps = [
        x_pad[a : a + length, b : b + length].reshape(cells, chan_full)
        for a in range(3)
        for b in range(3)
    ]
    one_local = jnp.stack(
        [
            lax.dot_general(
                pre_b, tap, (((0,), (0,)), ((), ())), preferred_element_type=jnp.float32
            )
            for tap in x_taps
        ]
    )
    small_rows = -(-(inner // chan_full + 1) // 8) * 8
    small = jnp.concatenate(
        [
            jnp.pad(bias_local, (0, (small_rows - 1) * chan_full - inner)),
            jnp.pad(loss_local[None], (0, chan_full - 1)),
        ]
    ).reshape(small_rows, chan_full)
    sum_two, sum_one, sum_small = sum_over_patches(
        two_local.reshape(9 * chan_full, inner), one_local.reshape(9 * inner, chan_full), small
    )
    grad_one = sum_one.reshape(9, inner, chan_full)
    grad_two = sum_two.reshape(9, chan_full, inner)
    grad_bias = sum_small[:-1].reshape(-1)[:inner]
    loss_value = sum_small[-1, 0] / (count * cells * chan_full * chans)
    return (loss_value, grad_one, grad_two, grad_bias)


def solution(mesh):
    placed = (
        P("patch", "chan", None),
        P(None, "chan", None),
        P("chan"),
        P(None, None, "chan"),
        P(),
        P(),
        P(),
        P("patch", "chan", None),
        P("patch", None),
    )
    return jax.shard_map(
        on_device,
        mesh=mesh,
        in_specs=placed,
        out_specs=(P(), P(None, "chan", None), P(None, None, "chan"), P("chan")),
        check_vma=False,
    )
```

```python
import math

import jax
import jax.numpy as jnp
from jax import lax
from jax.experimental import pallas as pl
from jax.experimental.pallas import tpu as pltpu
from jax.sharding import PartitionSpec as P

P_SIZE = 32


def edges_of(grid):
    return jnp.stack([grid[0], grid[-1], grid[:, 0], grid[:, -1]])


def with_frame(grid, strips):
    rows = jnp.concatenate([strips[0][None], grid, strips[1][None]], axis=0)
    left = jnp.pad(strips[2], ((1, 1), (0, 0)))[:, None]
    right = jnp.pad(strips[3], ((1, 1), (0, 0)))[:, None]
    return jnp.concatenate([left, rows, right], axis=1)


def conv(values, weight, pad, spec):
    return lax.conv_general_dilated(
        values[None],
        weight,
        (1, 1),
        ((pad, pad), (pad, pad)),
        dimension_numbers=("NHWC", spec, "NHWC"),
        preferred_element_type=jnp.float32,
    )[0]


def smooth_gate(values):
    return jax.nn.gelu(values, approximate=True)


def bits_of(size):
    return [1 << k for k in range(size.bit_length() - 1)]


def peer_of(place, bit):
    return place + bit - 2 * bit * (lax.div(place, bit) % 2)


def sum_kernel(count, chans, a_in, b_in, s_in, a_out, b_out, s_out, a_rec, b_rec, s_rec, send, recv):
    place = lax.axis_index("patch")
    lane = lax.axis_index("chan")
    bits = bits_of(count)
    swapped = bits if len(bits) < 3 else [bits[0], bits[2], bits[1]] + bits[3:]
    chan_bits = bits_of(chans)
    stages = len(bits)

    def target(bit):
        return {"patch": peer_of(place, bit)}

    barrier = pltpu.get_barrier_semaphore()
    for bit in bits:
        pl.semaphore_signal(
            barrier, inc=1, device_id=target(bit), device_id_type=pl.DeviceIdType.MESH
        )
    for bit in chan_bits:
        pl.semaphore_signal(
            barrier,
            inc=1,
            device_id={"chan": peer_of(lane, bit)},
            device_id_type=pl.DeviceIdType.MESH,
        )
    pl.semaphore_wait(barrier, stages + len(chan_bits))

    slot = [0]

    def send_to(src, dst, device):
        k = slot[0]
        slot[0] = k + 1
        copy = pltpu.make_async_remote_copy(
            src_ref=src,
            dst_ref=dst,
            send_sem=send.at[k],
            recv_sem=recv.at[k],
            device_id=device,
            device_id_type=pl.DeviceIdType.MESH,
        )
        copy.start()
        return copy

    def split(rows):
        units = rows // (8 * count)
        first = (units - units // 2) * 8 * count
        return [(0, first), (first, rows - first)] if units > 1 else [(0, rows)]

    s_out[...] = s_in[...]
    groups = [
        [
            {"in": held, "out": out, "rec": rec, "order": order, "start": low, "rows": rows,
             "base": low, "held": held, "at": low}
            for low, rows in split(held.shape[0])
        ]
        for held, out, rec, order in ((a_in, a_out, a_rec, bits), (b_in, b_out, b_rec, swapped))
    ]
    streams = groups[0][:1] + groups[1][:1] + groups[0][1:] + groups[1][1:]

    def scatter(one, stage):
        bit = one["order"][stage]
        half = one["rows"] // 2
        mine = lax.div(place, bit) % 2
        away = pl.multiple_of(one["at"] + (1 - mine) * half, 8)
        landing = one["rec"].at[pl.ds(one["base"], half)]
        one["copy"] = send_to(one["held"].at[pl.ds(away, half)], landing, target(bit))
        one["at"] = pl.multiple_of(one["at"] + mine * half, 8)
        one["start"] = one["start"] + mine * half
        one["rows"] = half

    def gather(one, stage):
        rows = one["rows"]
        bit = one["order"][stage]
        mine = lax.div(place, bit) % 2
        part = one["out"].at[pl.ds(pl.multiple_of(one["start"], 8), rows)]
        one["copy"] = send_to(part, part, target(bit))
        one["start"] = one["start"] - mine * rows
        one["rows"] = 2 * rows

    for one in streams:
        scatter(one, 0)
    small = send_to(s_out, s_rec.at[0], target(bits[0]))
    for stage in range(stages):
        for one in streams:
            one["copy"].wait()
            half = one["rows"]
            total = one["held"][pl.ds(one["at"], half)] + one["rec"][pl.ds(one["base"], half)]
            if stage == stages - 1:
                one["out"][pl.ds(pl.multiple_of(one["start"], 8), half)] = total
                gather(one, stage)
            else:
                one["rec"][pl.ds(one["base"], half)] = total
                one["held"] = one["rec"]
                one["at"] = one["base"]
                one["base"] += half
                scatter(one, stage + 1)
        small.wait()
        s_out[...] = s_out[...] + s_rec[stage]
        if stage + 1 < stages:
            small = send_to(s_out, s_rec.at[stage + 1], target(bits[stage + 1]))
    loss_row = lax.broadcasted_iota(jnp.int32, s_out.shape, 0) == s_out.shape[0] - 1
    for place_at, bit in enumerate(chan_bits):
        small = send_to(s_out, s_rec.at[stages + place_at], {"chan": peer_of(lane, bit)})
        small.wait()
        s_out[...] = s_out[...] + jnp.where(loss_row, s_rec[stages + place_at], 0.0)
    for stage in range(stages - 1, -1, -1):
        for one in streams:
            one["copy"].wait()
            if stage > 0:
                gather(one, stage - 1)


def sum_over_patches(a, b, small):
    count = lax.axis_size("patch")
    chans = lax.axis_size("chan")
    stages = len(bits_of(count))
    chan_stages = len(bits_of(chans))
    unit = 8 * count

    def padded(rows):
        return -(-rows // unit) * unit

    a_rows, b_rows = padded(a.shape[0]), padded(b.shape[0])
    a_full = jnp.pad(a, ((0, a_rows - a.shape[0]), (0, 0)))
    b_full = jnp.pad(b, ((0, b_rows - b.shape[0]), (0, 0)))
    copies = 9 * stages + chan_stages
    spec = pl.BlockSpec(memory_space=pltpu.VMEM)

    def kernel(*refs):
        sum_kernel(count, chans, *refs)

    a_sum, b_sum, s_sum = pl.pallas_call(
        kernel,
        out_shape=[
            jax.ShapeDtypeStruct(a_full.shape, jnp.float32),
            jax.ShapeDtypeStruct(b_full.shape, jnp.float32),
            jax.ShapeDtypeStruct(small.shape, jnp.float32),
        ],
        in_specs=[spec] * 3,
        out_specs=[spec] * 3,
        scratch_shapes=[
            pltpu.VMEM((a_rows, a.shape[1]), jnp.float32),
            pltpu.VMEM((b_rows, b.shape[1]), jnp.float32),
            pltpu.VMEM((stages + chan_stages,) + small.shape, jnp.float32),
            pltpu.SemaphoreType.DMA((copies,)),
            pltpu.SemaphoreType.DMA((copies,)),
        ],
        compiler_params=pltpu.CompilerParams(
            collective_id=0, has_side_effects=True, vmem_limit_bytes=24 << 20
        ),
    )(a_full, b_full, small)
    return a_sum[: a.shape[0]], b_sum[: b.shape[0]], s_sum


def on_device(fields, w_one, bias_one, w_two, neighbour, seam_code, band_order, target, lat_weight):
    length = P_SIZE
    cells = length * length
    count = lax.axis_size("patch")
    chans = lax.axis_size("chan")
    part = cells // count
    own = lax.axis_index("patch")
    own_nbr = lax.dynamic_slice_in_dim(neighbour, own, 1, 0)[0]
    own_code = lax.dynamic_slice_in_dim(seam_code, own, 1, 0)[0]
    ids = jnp.arange(count, dtype=jnp.int32)
    faces = (own_nbr[:, None] == ids[None, :]).astype(jnp.bfloat16)
    turned = (own_code >= 4)[:, None, None]
    inner = w_one.shape[1]

    def to_send(grid):
        strips = edges_of(grid)
        strips = jnp.where(turned, strips[:, ::-1], strips)
        return jnp.einsum(
            "tr,tkc->rkc", faces, strips, preferred_element_type=jnp.float32
        ).astype(jnp.bfloat16)

    def picked(arrived):
        return jnp.einsum(
            "tr,rkc->tkc", faces, arrived, preferred_element_type=jnp.float32
        ).astype(jnp.bfloat16)

    def swap(sent):
        return lax.all_to_all(sent, "patch", split_axis=0, concat_axis=0, tiled=True)

    both = lax.all_gather(jnp.stack([fields[0], target[0]]), "chan", axis=1, tiled=True)
    chan_full = both.shape[1]
    x_grid = both[0].T.reshape(length, length, chan_full)
    slots = (band_order[None, :] == ids[:, None]).astype(jnp.bfloat16)
    lat_rows = -(-part // chan_full)
    lat_parts = jnp.pad(
        lat_weight.reshape(count, part), ((0, 0), (0, lat_rows * chan_full - part))
    ).reshape(count, lat_rows, chan_full)
    band_parts = jnp.concatenate(
        [both[1].T.reshape(count, part, chan_full), lat_parts], axis=1
    )
    band_parts = jnp.einsum(
        "ps,skc->pkc", slots, band_parts, preferred_element_type=jnp.float32
    ).astype(jnp.bfloat16)
    first = swap(to_send(x_grid))
    band_parts, first = lax.optimization_barrier((band_parts, first))
    second = swap(band_parts)
    x_pad = with_frame(x_grid, picked(first))
    target_patch = second[:, :part].reshape(cells, chan_full)
    lat_w = (
        second[:, part:].reshape(count, lat_rows * chan_full)[:, :part].reshape(cells, 1)
    ).astype(jnp.float32)

    preact = conv(x_pad, w_one.reshape(3, 3, inner, chan_full), 0, "HWOI") + bias_one
    hidden = smooth_gate(preact).astype(jnp.bfloat16)
    h_pad = with_frame(hidden, picked(swap(to_send(hidden))))
    partial = conv(h_pad, w_two.reshape(3, 3, chan_full, inner), 0, "HWOI").reshape(
        cells, chan_full
    )
    mixed = partial
    rounded = partial.astype(jnp.bfloat16)
    for shift in range(1, chans):
        mixed = mixed + lax.ppermute(
            rounded, "chan", [(i, (i + shift) % chans) for i in range(chans)]
        ).astype(jnp.float32)
    x_flat = x_grid.reshape(cells, chan_full)
    misfit = x_flat.astype(jnp.float32) + mixed - target_patch.astype(jnp.float32)
    weighted = lat_w * misfit
    loss_local = jnp.sum(weighted * misfit)
    inv_root = 1.0 / math.sqrt(count * cells)
    grad_out = (weighted * inv_root).astype(jnp.bfloat16)
    g_grid = grad_out.reshape(length, length, chan_full)

    h_taps = [
        h_pad[a : a + length, b : b + length].reshape(cells, inner)
        for a in range(3)
        for b in range(3)
    ]
    two_local = jnp.stack(
        [
            lax.dot_general(
                grad_out, tap, (((0,), (0,)), ((), ())), preferred_element_type=jnp.float32
            )
            for tap in h_taps
        ]
    )

    near = picked(swap(to_send(g_grid)))
    side_taps = jnp.array([[0, 1, 2], [6, 7, 8], [0, 3, 6], [2, 5, 8]], jnp.int32)
    used = side_taps[own_code % 4]
    used = jnp.where((own_code >= 4)[:, None], used[:, ::-1], used)
    hot = (used[:, :, None] == jnp.arange(9)[None, None, :]).astype(jnp.bfloat16)
    spread = jnp.pad(near, ((0, 0), (1, 1), (0, 0)))
    shifted = jnp.stack([spread[:, 2 - d : 2 - d + length] for d in range(3)], axis=1)
    side_in = jnp.einsum(
        "tdn,tdkc->tknc", hot, shifted, preferred_element_type=jnp.float32
    ).astype(jnp.bfloat16)
    back = lax.dot_general(
        side_in.reshape(4 * length, 9 * chan_full),
        w_two.reshape(9 * chan_full, inner),
        (((1,), (0,)), ((), ())),
        preferred_element_type=jnp.float32,
    ).reshape(4, length, inner)
    grad_h = conv(g_grid, w_two.reshape(3, 3, chan_full, inner)[::-1, ::-1], 1, "HWIO")
    row = lax.broadcasted_iota(jnp.int32, (length, length, 1), 0)
    col = lax.broadcasted_iota(jnp.int32, (length, length, 1), 1)
    grad_h = (
        grad_h
        + jnp.where(row == 0, back[0][None], 0.0)
        + jnp.where(row == length - 1, back[1][None], 0.0)
        + jnp.where(col == 0, back[2][:, None], 0.0)
        + jnp.where(col == length - 1, back[3][:, None], 0.0)
    )
    grad_pre = jax.vjp(smooth_gate, preact)[1](grad_h)[0].reshape(cells, inner)
    bias_local = jnp.sum(grad_pre, axis=0)
    pre_b = grad_pre.astype(jnp.bfloat16)
    x_taps = [
        x_pad[a : a + length, b : b + length].reshape(cells, chan_full)
        for a in range(3)
        for b in range(3)
    ]
    one_local = jnp.stack(
        [
            lax.dot_general(
                pre_b, tap, (((0,), (0,)), ((), ())), preferred_element_type=jnp.float32
            )
            for tap in x_taps
        ]
    )
    small_rows = -(-(inner // chan_full + 1) // 8) * 8
    small = jnp.concatenate(
        [
            jnp.pad(bias_local, (0, (small_rows - 1) * chan_full - inner)),
            jnp.pad(loss_local[None], (0, chan_full - 1)),
        ]
    ).reshape(small_rows, chan_full)
    sum_two, sum_one, sum_small = sum_over_patches(
        two_local.reshape(9 * chan_full, inner), one_local.reshape(9 * inner, chan_full), small
    )
    grad_one = sum_one.reshape(9, inner, chan_full)
    grad_two = sum_two.reshape(9, chan_full, inner)
    grad_bias = sum_small[:-1].reshape(-1)[:inner]
    loss_value = sum_small[-1, 0] / (count * cells * chan_full * chans)
    return (loss_value, grad_one, grad_two, grad_bias)


def solution(mesh):
    placed = (
        P("patch", "chan", None),
        P(None, "chan", None),
        P("chan"),
        P(None, None, "chan"),
        P(),
        P(),
        P(),
        P("patch", "chan", None),
        P("patch", None),
    )
    return jax.shard_map(
        on_device,
        mesh=mesh,
        in_specs=placed,
        out_specs=(P(), P(None, "chan", None), P(None, None, "chan"), P("chan")),
        check_vma=False,
    )
```

```python
import math

import jax
import jax.numpy as jnp
from jax import lax
from jax.experimental import pallas as pl
from jax.experimental.pallas import tpu as pltpu
from jax.sharding import PartitionSpec as P

P_SIZE = 32


def edges_of(grid):
    return jnp.stack([grid[0], grid[-1], grid[:, 0], grid[:, -1]])


def with_frame(grid, strips):
    rows = jnp.concatenate([strips[0][None], grid, strips[1][None]], axis=0)
    left = jnp.pad(strips[2], ((1, 1), (0, 0)))[:, None]
    right = jnp.pad(strips[3], ((1, 1), (0, 0)))[:, None]
    return jnp.concatenate([left, rows, right], axis=1)


def conv(values, weight, pad, spec):
    return lax.conv_general_dilated(
        values[None],
        weight,
        (1, 1),
        ((pad, pad), (pad, pad)),
        dimension_numbers=("NHWC", spec, "NHWC"),
        preferred_element_type=jnp.float32,
    )[0]


def smooth_gate(values):
    return jax.nn.gelu(values, approximate=True)


def bits_of(size):
    return [1 << k for k in range(size.bit_length() - 1)]


def peer_of(place, bit):
    return place + bit - 2 * bit * (lax.div(place, bit) % 2)


def sum_kernel(count, chans, a_in, b_in, s_in, a_out, b_out, s_out, a_rec, b_rec, s_rec, send, recv):
    place = lax.axis_index("patch")
    lane = lax.axis_index("chan")
    bits = bits_of(count)
    swapped = bits if len(bits) < 3 else [bits[0], bits[2], bits[1]] + bits[3:]
    chan_bits = bits_of(chans)
    stages = len(bits)

    def target(bit):
        return {"patch": peer_of(place, bit)}

    barrier = pltpu.get_barrier_semaphore()
    for bit in bits:
        pl.semaphore_signal(
            barrier, inc=1, device_id=target(bit), device_id_type=pl.DeviceIdType.MESH
        )
    for bit in chan_bits:
        pl.semaphore_signal(
            barrier,
            inc=1,
            device_id={"chan": peer_of(lane, bit)},
            device_id_type=pl.DeviceIdType.MESH,
        )
    pl.semaphore_wait(barrier, stages + len(chan_bits))

    slot = [0]

    def send_to(src, dst, device):
        k = slot[0]
        slot[0] = k + 1
        copy = pltpu.make_async_remote_copy(
            src_ref=src,
            dst_ref=dst,
            send_sem=send.at[k],
            recv_sem=recv.at[k],
            device_id=device,
            device_id_type=pl.DeviceIdType.MESH,
        )
        copy.start()
        return copy

    def split(rows):
        units = rows // (8 * count)
        first = (units - units // 2) * 8 * count
        return [(0, first), (first, rows - first)] if units > 1 else [(0, rows)]

    s_out[...] = s_in[...]
    groups = [
        [
            {"in": held, "out": out, "rec": rec, "order": order, "start": low, "rows": rows,
             "base": low, "held": held, "at": low}
            for low, rows in split(held.shape[0])
        ]
        for held, out, rec, order in ((a_in, a_out, a_rec, bits), (b_in, b_out, b_rec, swapped))
    ]
    streams = groups[0][:1] + groups[1][:1] + groups[0][1:] + groups[1][1:]

    def scatter(one, stage):
        bit = one["order"][stage]
        half = one["rows"] // 2
        mine = lax.div(place, bit) % 2
        away = pl.multiple_of(one["at"] + (1 - mine) * half, 8)
        landing = one["rec"].at[pl.ds(one["base"], half)]
        one["copy"] = send_to(one["held"].at[pl.ds(away, half)], landing, target(bit))
        one["at"] = pl.multiple_of(one["at"] + mine * half, 8)
        one["start"] = one["start"] + mine * half
        one["rows"] = half

    def gather(one, stage):
        rows = one["rows"]
        bit = one["order"][stage]
        mine = lax.div(place, bit) % 2
        part = one["out"].at[pl.ds(pl.multiple_of(one["start"], 8), rows)]
        one["copy"] = send_to(part, part, target(bit))
        one["start"] = one["start"] - mine * rows
        one["rows"] = 2 * rows

    for one in streams:
        scatter(one, 0)
    small = send_to(s_out, s_rec.at[0], target(bits[0]))
    for stage in range(stages):
        for one in streams:
            one["copy"].wait()
            half = one["rows"]
            total = one["held"][pl.ds(one["at"], half)] + one["rec"][pl.ds(one["base"], half)]
            if stage == stages - 1:
                one["out"][pl.ds(pl.multiple_of(one["start"], 8), half)] = total
                gather(one, stage)
            else:
                one["rec"][pl.ds(one["base"], half)] = total
                one["held"] = one["rec"]
                one["at"] = one["base"]
                one["base"] += half
                scatter(one, stage + 1)
        small.wait()
        s_out[...] = s_out[...] + s_rec[stage]
        if stage + 1 < stages:
            small = send_to(s_out, s_rec.at[stage + 1], target(bits[stage + 1]))
    loss_row = lax.broadcasted_iota(jnp.int32, s_out.shape, 0) == s_out.shape[0] - 1
    for place_at, bit in enumerate(chan_bits):
        small = send_to(s_out, s_rec.at[stages + place_at], {"chan": peer_of(lane, bit)})
        small.wait()
        s_out[...] = s_out[...] + jnp.where(loss_row, s_rec[stages + place_at], 0.0)
    for stage in range(stages - 1, -1, -1):
        for one in streams:
            one["copy"].wait()
            if stage > 0:
                gather(one, stage - 1)


def sum_over_patches(a, b, small):
    count = lax.axis_size("patch")
    chans = lax.axis_size("chan")
    stages = len(bits_of(count))
    chan_stages = len(bits_of(chans))
    unit = 8 * count

    def padded(rows):
        return -(-rows // unit) * unit

    a_rows, b_rows = padded(a.shape[0]), padded(b.shape[0])
    a_full = jnp.pad(a, ((0, a_rows - a.shape[0]), (0, 0)))
    b_full = jnp.pad(b, ((0, b_rows - b.shape[0]), (0, 0)))
    copies = 9 * stages + chan_stages
    spec = pl.BlockSpec(memory_space=pltpu.VMEM)

    def kernel(*refs):
        sum_kernel(count, chans, *refs)

    a_sum, b_sum, s_sum = pl.pallas_call(
        kernel,
        out_shape=[
            jax.ShapeDtypeStruct(a_full.shape, jnp.float32),
            jax.ShapeDtypeStruct(b_full.shape, jnp.float32),
            jax.ShapeDtypeStruct(small.shape, jnp.float32),
        ],
        in_specs=[spec] * 3,
        out_specs=[spec] * 3,
        scratch_shapes=[
            pltpu.VMEM((a_rows, a.shape[1]), jnp.float32),
            pltpu.VMEM((b_rows, b.shape[1]), jnp.float32),
            pltpu.VMEM((stages + chan_stages,) + small.shape, jnp.float32),
            pltpu.SemaphoreType.DMA((copies,)),
            pltpu.SemaphoreType.DMA((copies,)),
        ],
        compiler_params=pltpu.CompilerParams(
            collective_id=0, has_side_effects=True, vmem_limit_bytes=24 << 20
        ),
    )(a_full, b_full, small)
    return a_sum[: a.shape[0]], b_sum[: b.shape[0]], s_sum


def on_device(fields, w_one, bias_one, w_two, neighbour, seam_code, band_order, target, lat_weight):
    length = P_SIZE
    cells = length * length
    count = lax.axis_size("patch")
    chans = lax.axis_size("chan")
    part = cells // count
    own = lax.axis_index("patch")
    own_nbr = lax.dynamic_slice_in_dim(neighbour, own, 1, 0)[0]
    own_code = lax.dynamic_slice_in_dim(seam_code, own, 1, 0)[0]
    ids = jnp.arange(count, dtype=jnp.int32)
    faces = (own_nbr[:, None] == ids[None, :]).astype(jnp.bfloat16)
    turned = (own_code >= 4)[:, None, None]
    inner = w_one.shape[1]

    def to_send(grid):
        strips = edges_of(grid)
        strips = jnp.where(turned, strips[:, ::-1], strips)
        return jnp.einsum(
            "tr,tkc->rkc", faces, strips, preferred_element_type=jnp.float32
        ).astype(jnp.bfloat16)

    def picked(arrived):
        return jnp.einsum(
            "tr,rkc->tkc", faces, arrived, preferred_element_type=jnp.float32
        ).astype(jnp.bfloat16)

    def swap(sent):
        return lax.all_to_all(sent, "patch", split_axis=0, concat_axis=0, tiled=True)

    whole = lax.all_gather(fields[0], "chan", axis=0, tiled=True)
    chan_full = whole.shape[0]
    chan_own = fields.shape[1]
    x_grid = whole.T.reshape(length, length, chan_full)
    slots = (band_order[None, :] == ids[:, None]).astype(jnp.bfloat16)
    lat_rows = -(-part // chan_own)
    lat_parts = jnp.pad(
        lat_weight.reshape(count, part), ((0, 0), (0, lat_rows * chan_own - part))
    ).reshape(count, lat_rows, chan_own)
    band_parts = jnp.concatenate([target[0].T.reshape(count, part, chan_own), lat_parts], axis=1)
    band_parts = jnp.einsum(
        "ps,skc->pkc", slots, band_parts, preferred_element_type=jnp.float32
    ).astype(jnp.bfloat16)
    first = swap(to_send(x_grid))
    band_parts, first = lax.optimization_barrier((band_parts, first))
    second = swap(band_parts)
    x_pad = with_frame(x_grid, picked(first))
    lane = lax.axis_index("chan")
    pieces = [second[:, :part].reshape(cells, chan_own)]
    for shift in range(1, chans):
        pieces.append(
            lax.ppermute(pieces[0], "chan", [(i, (i + shift) % chans) for i in range(chans)])
        )
    target_patch = jnp.concatenate(
        [lax.select_n((lane - c + chans) % chans, *pieces) for c in range(chans)], axis=1
    )
    lat_w = (
        second[:, part:].reshape(count, lat_rows * chan_own)[:, :part].reshape(cells, 1)
    ).astype(jnp.float32)

    preact = conv(x_pad, w_one.reshape(3, 3, inner, chan_full), 0, "HWOI") + bias_one
    hidden = smooth_gate(preact).astype(jnp.bfloat16)
    h_pad = with_frame(hidden, picked(swap(to_send(hidden))))
    partial = conv(h_pad, w_two.reshape(3, 3, chan_full, inner), 0, "HWOI").reshape(
        cells, chan_full
    )
    mixed = partial
    rounded = partial.astype(jnp.bfloat16)
    for shift in range(1, chans):
        mixed = mixed + lax.ppermute(
            rounded, "chan", [(i, (i + shift) % chans) for i in range(chans)]
        ).astype(jnp.float32)
    x_flat = x_grid.reshape(cells, chan_full)
    misfit = x_flat.astype(jnp.float32) + mixed - target_patch.astype(jnp.float32)
    weighted = lat_w * misfit
    loss_local = jnp.sum(weighted * misfit)
    inv_root = 1.0 / math.sqrt(count * cells)
    grad_out = (weighted * inv_root).astype(jnp.bfloat16)
    g_grid = grad_out.reshape(length, length, chan_full)

    h_taps = [
        h_pad[a : a + length, b : b + length].reshape(cells, inner)
        for a in range(3)
        for b in range(3)
    ]
    two_local = jnp.stack(
        [
            lax.dot_general(
                grad_out, tap, (((0,), (0,)), ((), ())), preferred_element_type=jnp.float32
            )
            for tap in h_taps
        ]
    )

    near = picked(swap(to_send(g_grid)))
    side_taps = jnp.array([[0, 1, 2], [6, 7, 8], [0, 3, 6], [2, 5, 8]], jnp.int32)
    used = side_taps[own_code % 4]
    used = jnp.where((own_code >= 4)[:, None], used[:, ::-1], used)
    hot = (used[:, :, None] == jnp.arange(9)[None, None, :]).astype(jnp.bfloat16)
    spread = jnp.pad(near, ((0, 0), (1, 1), (0, 0)))
    shifted = jnp.stack([spread[:, 2 - d : 2 - d + length] for d in range(3)], axis=1)
    side_in = jnp.einsum(
        "tdn,tdkc->tknc", hot, shifted, preferred_element_type=jnp.float32
    ).astype(jnp.bfloat16)
    back = lax.dot_general(
        side_in.reshape(4 * length, 9 * chan_full),
        w_two.reshape(9 * chan_full, inner),
        (((1,), (0,)), ((), ())),
        preferred_element_type=jnp.float32,
    ).reshape(4, length, inner)
    grad_h = conv(g_grid, w_two.reshape(3, 3, chan_full, inner)[::-1, ::-1], 1, "HWIO")
    row = lax.broadcasted_iota(jnp.int32, (length, length, 1), 0)
    col = lax.broadcasted_iota(jnp.int32, (length, length, 1), 1)
    grad_h = (
        grad_h
        + jnp.where(row == 0, back[0][None], 0.0)
        + jnp.where(row == length - 1, back[1][None], 0.0)
        + jnp.where(col == 0, back[2][:, None], 0.0)
        + jnp.where(col == length - 1, back[3][:, None], 0.0)
    )
    grad_pre = jax.vjp(smooth_gate, preact)[1](grad_h)[0].reshape(cells, inner)
    bias_local = jnp.sum(grad_pre, axis=0)
    pre_b = grad_pre.astype(jnp.bfloat16)
    x_taps = [
        x_pad[a : a + length, b : b + length].reshape(cells, chan_full)
        for a in range(3)
        for b in range(3)
    ]
    one_local = jnp.stack(
        [
            lax.dot_general(
                pre_b, tap, (((0,), (0,)), ((), ())), preferred_element_type=jnp.float32
            )
            for tap in x_taps
        ]
    )
    small_rows = -(-(inner // chan_full + 1) // 8) * 8
    small = jnp.concatenate(
        [
            jnp.pad(bias_local, (0, (small_rows - 1) * chan_full - inner)),
            jnp.pad(loss_local[None], (0, chan_full - 1)),
        ]
    ).reshape(small_rows, chan_full)
    sum_two, sum_one, sum_small = sum_over_patches(
        two_local.reshape(9 * chan_full, inner), one_local.reshape(9 * inner, chan_full), small
    )
    grad_one = sum_one.reshape(9, inner, chan_full)
    grad_two = sum_two.reshape(9, chan_full, inner)
    grad_bias = sum_small[:-1].reshape(-1)[:inner]
    loss_value = sum_small[-1, 0] / (count * cells * chan_full * chans)
    return (loss_value, grad_one, grad_two, grad_bias)


def solution(mesh):
    placed = (
        P("patch", "chan", None),
        P(None, "chan", None),
        P("chan"),
        P(None, None, "chan"),
        P(),
        P(),
        P(),
        P("patch", "chan", None),
        P("patch", None),
    )
    return jax.shard_map(
        on_device,
        mesh=mesh,
        in_specs=placed,
        out_specs=(P(), P(None, "chan", None), P(None, None, "chan"), P("chan")),
        check_vma=False,
    )
```

```python
import math

import jax
import jax.numpy as jnp
from jax import lax
from jax.experimental import pallas as pl
from jax.experimental.pallas import tpu as pltpu
from jax.sharding import PartitionSpec as P

P_SIZE = 32


def edges_of(grid):
    return jnp.stack([grid[0], grid[-1], grid[:, 0], grid[:, -1]])


def with_frame(grid, strips):
    rows = jnp.concatenate([strips[0][None], grid, strips[1][None]], axis=0)
    left = jnp.pad(strips[2], ((1, 1), (0, 0)))[:, None]
    right = jnp.pad(strips[3], ((1, 1), (0, 0)))[:, None]
    return jnp.concatenate([left, rows, right], axis=1)


def conv(values, weight, pad, spec):
    return lax.conv_general_dilated(
        values[None],
        weight,
        (1, 1),
        ((pad, pad), (pad, pad)),
        dimension_numbers=("NHWC", spec, "NHWC"),
        preferred_element_type=jnp.float32,
    )[0]


def smooth_gate(values):
    return jax.nn.gelu(values, approximate=True)


def bits_of(size):
    return [1 << k for k in range(size.bit_length() - 1)]


def peer_of(place, bit):
    return place + bit - 2 * bit * (lax.div(place, bit) % 2)


def sum_kernel(
    count, chans, a_in, pre, taps, s_in, a_out, b_out, s_out, b_in, a_rec, b_rec, s_rec, send, recv
):
    place = lax.axis_index("patch")
    lane = lax.axis_index("chan")
    bits = bits_of(count)
    swapped = bits if len(bits) < 3 else [bits[0], bits[2], bits[1]] + bits[3:]
    chan_bits = bits_of(chans)
    stages = len(bits)

    def target(bit):
        return {"patch": peer_of(place, bit)}

    barrier = pltpu.get_barrier_semaphore()
    for bit in bits:
        pl.semaphore_signal(
            barrier, inc=1, device_id=target(bit), device_id_type=pl.DeviceIdType.MESH
        )
    for bit in chan_bits:
        pl.semaphore_signal(
            barrier,
            inc=1,
            device_id={"chan": peer_of(lane, bit)},
            device_id_type=pl.DeviceIdType.MESH,
        )
    pl.semaphore_wait(barrier, stages + len(chan_bits))

    slot = [0]

    def send_to(src, dst, device):
        k = slot[0]
        slot[0] = k + 1
        copy = pltpu.make_async_remote_copy(
            src_ref=src,
            dst_ref=dst,
            send_sem=send.at[k],
            recv_sem=recv.at[k],
            device_id=device,
            device_id_type=pl.DeviceIdType.MESH,
        )
        copy.start()
        return copy

    def split(rows):
        units = rows // (8 * count)
        first = (units - units // 2) * 8 * count
        return [(0, first), (first, rows - first)] if units > 1 else [(0, rows)]

    s_out[...] = s_in[...]
    groups = [
        [
            {"in": held, "out": out, "rec": rec, "order": order, "start": low, "rows": rows,
             "base": low, "held": held, "at": low}
            for low, rows in split(held.shape[0])
        ]
        for held, out, rec, order in ((a_in, a_out, a_rec, bits), (b_in, b_out, b_rec, swapped))
    ]
    streams = groups[0][:1] + groups[1][:1] + groups[0][1:] + groups[1][1:]

    def scatter(one, stage):
        bit = one["order"][stage]
        half = one["rows"] // 2
        mine = lax.div(place, bit) % 2
        away = pl.multiple_of(one["at"] + (1 - mine) * half, 8)
        landing = one["rec"].at[pl.ds(one["base"], half)]
        one["copy"] = send_to(one["held"].at[pl.ds(away, half)], landing, target(bit))
        one["at"] = pl.multiple_of(one["at"] + mine * half, 8)
        one["start"] = one["start"] + mine * half
        one["rows"] = half

    def gather(one, stage):
        rows = one["rows"]
        bit = one["order"][stage]
        mine = lax.div(place, bit) % 2
        part = one["out"].at[pl.ds(pl.multiple_of(one["start"], 8), rows)]
        one["copy"] = send_to(part, part, target(bit))
        one["start"] = one["start"] - mine * rows
        one["rows"] = 2 * rows

    inner = pre.shape[1]

    def products(low, high):
        for tap in range(low, high):
            rows = taps[tap % 3, tap // 3 : tap // 3 + P_SIZE]
            b_in[pl.ds(tap * inner, inner)] = lax.dot_general(
                pre[...],
                rows.reshape(P_SIZE * P_SIZE, rows.shape[-1]),
                (((0,), (0,)), ((), ())),
                preferred_element_type=jnp.float32,
            )

    for one in groups[0]:
        scatter(one, 0)
    done = 0
    if b_in.shape[0] > 9 * inner:
        b_in[pl.ds(9 * inner, b_in.shape[0] - 9 * inner)] = jnp.zeros(
            (b_in.shape[0] - 9 * inner, b_in.shape[1]), jnp.float32
        )
    for one in groups[1]:
        due = min(9, -(-(one["at"] + one["rows"]) // inner))
        products(done, due)
        done = due
        scatter(one, 0)
    small = send_to(s_out, s_rec.at[0], target(bits[0]))
    for stage in range(stages):
        for one in streams:
            one["copy"].wait()
            half = one["rows"]
            total = one["held"][pl.ds(one["at"], half)] + one["rec"][pl.ds(one["base"], half)]
            if stage == stages - 1:
                one["out"][pl.ds(pl.multiple_of(one["start"], 8), half)] = total
                gather(one, stage)
            else:
                one["rec"][pl.ds(one["base"], half)] = total
                one["held"] = one["rec"]
                one["at"] = one["base"]
                one["base"] += half
                scatter(one, stage + 1)
        small.wait()
        s_out[...] = s_out[...] + s_rec[stage]
        if stage + 1 < stages:
            small = send_to(s_out, s_rec.at[stage + 1], target(bits[stage + 1]))
    loss_row = lax.broadcasted_iota(jnp.int32, s_out.shape, 0) == s_out.shape[0] - 1
    for place_at, bit in enumerate(chan_bits):
        small = send_to(s_out, s_rec.at[stages + place_at], {"chan": peer_of(lane, bit)})
        small.wait()
        s_out[...] = s_out[...] + jnp.where(loss_row, s_rec[stages + place_at], 0.0)
    for stage in range(stages - 1, -1, -1):
        for one in streams:
            one["copy"].wait()
            if stage > 0:
                gather(one, stage - 1)


def sum_over_patches(a, pre, taps, small):
    count = lax.axis_size("patch")
    chans = lax.axis_size("chan")
    stages = len(bits_of(count))
    chan_stages = len(bits_of(chans))
    unit = 8 * count

    def padded(rows):
        return -(-rows // unit) * unit

    a_rows, b_rows = padded(a.shape[0]), padded(9 * pre.shape[1])
    a_full = jnp.pad(a, ((0, a_rows - a.shape[0]), (0, 0)))
    b_shape = (b_rows, taps.shape[-1])
    copies = 9 * stages + chan_stages
    spec = pl.BlockSpec(memory_space=pltpu.VMEM)

    def kernel(*refs):
        sum_kernel(count, chans, *refs)

    a_sum, b_sum, s_sum = pl.pallas_call(
        kernel,
        out_shape=[
            jax.ShapeDtypeStruct(a_full.shape, jnp.float32),
            jax.ShapeDtypeStruct(b_shape, jnp.float32),
            jax.ShapeDtypeStruct(small.shape, jnp.float32),
        ],
        in_specs=[spec] * 4,
        out_specs=[spec] * 3,
        scratch_shapes=[
            pltpu.VMEM(b_shape, jnp.float32),
            pltpu.VMEM((a_rows, a.shape[1]), jnp.float32),
            pltpu.VMEM(b_shape, jnp.float32),
            pltpu.VMEM((stages + chan_stages,) + small.shape, jnp.float32),
            pltpu.SemaphoreType.DMA((copies,)),
            pltpu.SemaphoreType.DMA((copies,)),
        ],
        compiler_params=pltpu.CompilerParams(
            collective_id=0, has_side_effects=True, vmem_limit_bytes=24 << 20
        ),
    )(a_full, pre, taps, small)
    return a_sum[: a.shape[0]], b_sum[: 9 * pre.shape[1]], s_sum


def on_device(fields, w_one, bias_one, w_two, neighbour, seam_code, band_order, target, lat_weight):
    length = P_SIZE
    cells = length * length
    count = lax.axis_size("patch")
    chans = lax.axis_size("chan")
    part = cells // count
    own = lax.axis_index("patch")
    own_nbr = lax.dynamic_slice_in_dim(neighbour, own, 1, 0)[0]
    own_code = lax.dynamic_slice_in_dim(seam_code, own, 1, 0)[0]
    ids = jnp.arange(count, dtype=jnp.int32)
    faces = (own_nbr[:, None] == ids[None, :]).astype(jnp.bfloat16)
    turned = (own_code >= 4)[:, None, None]
    inner = w_one.shape[1]

    def to_send(grid):
        strips = edges_of(grid)
        strips = jnp.where(turned, strips[:, ::-1], strips)
        return jnp.einsum(
            "tr,tkc->rkc", faces, strips, preferred_element_type=jnp.float32
        ).astype(jnp.bfloat16)

    def picked(arrived):
        return jnp.einsum(
            "tr,rkc->tkc", faces, arrived, preferred_element_type=jnp.float32
        ).astype(jnp.bfloat16)

    def swap(sent):
        return lax.all_to_all(sent, "patch", split_axis=0, concat_axis=0, tiled=True)

    lane = lax.axis_index("chan")
    pieces = [target[0]]
    for shift in range(1, chans):
        pieces.append(
            lax.ppermute(target[0], "chan", [(i, (i + shift) % chans) for i in range(chans)])
        )
    target_full = jnp.concatenate(
        [lax.select_n((lane - c + chans) % chans, *pieces) for c in range(chans)], axis=0
    )
    whole = lax.all_gather(fields[0], "chan", axis=0, tiled=True)
    chan_full = whole.shape[0]
    x_grid = whole.T.reshape(length, length, chan_full)
    slots = (band_order[None, :] == ids[:, None]).astype(jnp.bfloat16)
    lat_rows = -(-part // chan_full)
    lat_parts = jnp.pad(
        lat_weight.reshape(count, part), ((0, 0), (0, lat_rows * chan_full - part))
    ).reshape(count, lat_rows, chan_full)
    band_parts = jnp.concatenate(
        [target_full.T.reshape(count, part, chan_full), lat_parts], axis=1
    )
    band_parts = jnp.einsum(
        "ps,skc->pkc", slots, band_parts, preferred_element_type=jnp.float32
    ).astype(jnp.bfloat16)
    first = swap(to_send(x_grid))
    band_parts, first = lax.optimization_barrier((band_parts, first))
    second = swap(band_parts)
    x_pad = with_frame(x_grid, picked(first))
    target_patch = second[:, :part].reshape(cells, chan_full)
    lat_w = (
        second[:, part:].reshape(count, lat_rows * chan_full)[:, :part].reshape(cells, 1)
    ).astype(jnp.float32)

    preact = conv(x_pad, w_one.reshape(3, 3, inner, chan_full), 0, "HWOI") + bias_one
    hidden = smooth_gate(preact).astype(jnp.bfloat16)
    h_pad = with_frame(hidden, picked(swap(to_send(hidden))))
    partial = conv(h_pad, w_two.reshape(3, 3, chan_full, inner), 0, "HWOI").reshape(
        cells, chan_full
    )
    mixed = partial
    rounded = partial.astype(jnp.bfloat16)
    for shift in range(1, chans):
        mixed = mixed + lax.ppermute(
            rounded, "chan", [(i, (i + shift) % chans) for i in range(chans)]
        ).astype(jnp.float32)
    x_flat = x_grid.reshape(cells, chan_full)
    misfit = x_flat.astype(jnp.float32) + mixed - target_patch.astype(jnp.float32)
    weighted = lat_w * misfit
    loss_local = jnp.sum(weighted * misfit)
    inv_root = 1.0 / math.sqrt(count * cells)
    grad_out = (weighted * inv_root).astype(jnp.bfloat16)
    g_grid = grad_out.reshape(length, length, chan_full)

    h_taps = [
        h_pad[a : a + length, b : b + length].reshape(cells, inner)
        for a in range(3)
        for b in range(3)
    ]
    two_local = jnp.stack(
        [
            lax.dot_general(
                grad_out, tap, (((0,), (0,)), ((), ())), preferred_element_type=jnp.float32
            )
            for tap in h_taps
        ]
    )

    near = picked(swap(to_send(g_grid)))
    side_taps = jnp.array([[0, 1, 2], [6, 7, 8], [0, 3, 6], [2, 5, 8]], jnp.int32)
    used = side_taps[own_code % 4]
    used = jnp.where((own_code >= 4)[:, None], used[:, ::-1], used)
    hot = (used[:, :, None] == jnp.arange(9)[None, None, :]).astype(jnp.bfloat16)
    spread = jnp.pad(near, ((0, 0), (1, 1), (0, 0)))
    shifted = jnp.stack([spread[:, 2 - d : 2 - d + length] for d in range(3)], axis=1)
    side_in = jnp.einsum(
        "tdn,tdkc->tknc", hot, shifted, preferred_element_type=jnp.float32
    ).astype(jnp.bfloat16)
    back = lax.dot_general(
        side_in.reshape(4 * length, 9 * chan_full),
        w_two.reshape(9 * chan_full, inner),
        (((1,), (0,)), ((), ())),
        preferred_element_type=jnp.float32,
    ).reshape(4, length, inner)
    grad_h = conv(g_grid, w_two.reshape(3, 3, chan_full, inner)[::-1, ::-1], 1, "HWIO")
    row = lax.broadcasted_iota(jnp.int32, (length, length, 1), 0)
    col = lax.broadcasted_iota(jnp.int32, (length, length, 1), 1)
    grad_h = (
        grad_h
        + jnp.where(row == 0, back[0][None], 0.0)
        + jnp.where(row == length - 1, back[1][None], 0.0)
        + jnp.where(col == 0, back[2][:, None], 0.0)
        + jnp.where(col == length - 1, back[3][:, None], 0.0)
    )
    grad_pre = jax.vjp(smooth_gate, preact)[1](grad_h)[0].reshape(cells, inner)
    bias_local = jnp.sum(grad_pre, axis=0)
    pre_b = grad_pre.astype(jnp.bfloat16)
    x_taps = jnp.stack([x_pad[:, b : b + length] for b in range(3)])
    small_rows = -(-(inner // chan_full + 1) // 8) * 8
    small = jnp.concatenate(
        [
            jnp.pad(bias_local, (0, (small_rows - 1) * chan_full - inner)),
            jnp.pad(loss_local[None], (0, chan_full - 1)),
        ]
    ).reshape(small_rows, chan_full)
    sum_two, sum_one, sum_small = sum_over_patches(
        two_local.reshape(9 * chan_full, inner), pre_b, x_taps, small
    )
    grad_one = sum_one.reshape(9, inner, chan_full)
    grad_two = sum_two.reshape(9, chan_full, inner)
    grad_bias = sum_small[:-1].reshape(-1)[:inner]
    loss_value = sum_small[-1, 0] / (count * cells * chan_full * chans)
    return (loss_value, grad_one, grad_two, grad_bias)


def solution(mesh):
    placed = (
        P("patch", "chan", None),
        P(None, "chan", None),
        P("chan"),
        P(None, None, "chan"),
        P(),
        P(),
        P(),
        P("patch", "chan", None),
        P("patch", None),
    )
    return jax.shard_map(
        on_device,
        mesh=mesh,
        in_specs=placed,
        out_specs=(P(), P(None, "chan", None), P(None, None, "chan"), P("chan")),
        check_vma=False,
    )
```
